256 devices in a mesh: gx: 16 (over z, x_hi), gy: 8 (over y, x_lo), gz: 2 (over core).
Axes of the slice: x: 4 (x_hi: 2, x_lo: 2; x = x_hi * 2 + x_lo), y: 4, z: 8, core: 2. Of those that a mesh axis runs over, the one named last changes fastest.
Arguments:
- forward: float32 [19, 256, 128, 256], P(None, 'gx', 'gy', 'gz'), may hold values from 0.01 to 0.15
- adjoint: float32 [19, 256, 128, 256], P(None, 'gx', 'gy', 'gz'), may hold values from -1.2 to 1.2
- design: float32 [256, 128, 256], P('gx', 'gy', 'gz'), may hold values from 0 to 1
- mask: int32 [256, 128, 256], P('gx', 'gy', 'gz'), may hold values from 0 to 3
Outputs:
- adjoint_next: float32 [19, 256, 128, 256], P(None, 'gx', 'gy', 'gz')
- sensitivity: float32 [256, 128, 256], P('gx', 'gy', 'gz')
The draws below stay inside these ranges and needn't reach their ends.
All inputs are finite; a program needn't handle non-finite values.
Results may differ from the reference program's by a relative error of at most 0.0003.
Values sent between devices are 32-bit elements; how exact they have to be, the bound alone decides.
A program may use at most 64 MiB of HBM per device.

```python
import math
import jax
import jax.numpy as jnp
from jax import lax

Q = 19
RADIUS = 8
NX = 256
NY = 128
NZ = 256


def touch_ends(array, rng, low, largest):
    spot = [jax.random.randint(jax.random.fold_in(rng, axis), (), 0, length) for axis, length in enumerate(array.shape)]
    longest = array.shape.index(max(array.shape))
    neighbour = spot[:longest] + [(spot[longest] + 1) % array.shape[longest]] + spot[longest + 1:]
    return array.at[tuple(spot)].set(low).at[tuple(neighbour)].set(largest)


def level_of(key, shape, pieces, smallest, largest):
    def one(dim, blocks):
        steps = jax.random.uniform(jax.random.fold_in(jax.random.fold_in(key, 6), dim), (blocks,), jnp.float32, smallest / len(pieces), largest / len(pieces))
        return jnp.repeat(jnp.exp(steps), shape[dim] // blocks).reshape((-1,) + (1,) * (len(shape) - dim - 1))

    loudness = one(*pieces[0])
    for cut in pieces[1:]:
        loudness = loudness * one(*cut)
    return loudness


def gaussian(own_key, shape, width, limit, split=(), dtype=jnp.bfloat16):
    array = jax.random.normal(own_key, shape, jnp.float32) * width
    if len(split) > 0:
        array = level_of(own_key, shape, split, -0.22, 0.18) * array
    return jnp.clip(array, min=-limit, max=limit).astype(dtype)


def setup_inputs(seed: int = 0) -> dict:
    streams_of = jax.random.split(jax.random.key(seed), 5)
    forward = jnp.clip(0.01 + 0.14 * jax.random.uniform(streams_of[0], (Q, NX, NY, NZ), jnp.float32) ** level_of(streams_of[0], (Q, NX, NY, NZ), ((1, 16), (2, 8), (3, 2)), -0.2, 0.2), 0.01, 0.15)
    adjoint = gaussian(streams_of[1], (Q, NX, NY, NZ), 0.2, 1.2, ((1, 16), (2, 8), (3, 2)), jnp.float32)
    design = jnp.clip(1.0 * jax.random.uniform(streams_of[2], (NX, NY, NZ), jnp.float32) ** level_of(streams_of[2], (NX, NY, NZ), ((0, 16), (1, 8), (2, 2)), -0.2, 0.2), 0.0, 1.0)
    mask = touch_ends(jax.random.randint(streams_of[3], (NX, NY, NZ), 0, 4), jax.random.fold_in(streams_of[3], 1), 0, 3).astype(jnp.int32)
    return dict(forward=forward, adjoint=adjoint, design=design, mask=mask)


velocity = [(0, 0, 0), (1, 0, 0), (-1, 0, 0), (0, 1, 0), (0, -1, 0), (0, 0, 1), (0, 0, -1),
            (1, 1, 0), (-1, -1, 0), (1, -1, 0), (-1, 1, 0), (1, 0, 1), (-1, 0, -1),
            (1, 0, -1), (-1, 0, 1), (0, 1, 1), (0, -1, -1), (0, 1, -1), (0, -1, 1)]
lattice_weight = [1.0 / 3.0] + [1.0 / 18.0] * 6 + [1.0 / 36.0] * 12
opposite = [0, 2, 1, 4, 3, 6, 5, 8, 7, 10, 9, 12, 11, 14, 13, 16, 15, 18, 17]
relax_rate = 1.25
sharpness = 64.0
threshold = 0.5
damping_max = 10.0
ramp_shape = 0.1


def tap_weights():
    spread_width = RADIUS / 2.0
    unscaled = [math.exp(-((k - RADIUS) ** 2) / (2.0 * spread_width * spread_width)) for k in range(2 * RADIUS + 1)]
    summed = sum(unscaled)
    return [v / summed for v in unscaled]


def filter_along(padded, along, length_out):
    weights = tap_weights()
    result = weights[0] * lax.slice_in_dim(padded, 0, length_out, axis=along)
    for k in range(1, 2 * RADIUS + 1):
        result = result + weights[k] * lax.slice_in_dim(padded, k, k + length_out, axis=along)
    return result


def smooth(field):
    for along in range(3):
        widths = [(0, 0), (0, 0), (0, 0)]
        widths[along] = (RADIUS, RADIUS)
        field = filter_along(jnp.pad(field, widths), along, field.shape[along])
    return field


def project(filtered):
    base = math.tanh(sharpness * threshold)
    denominator = base + math.tanh(sharpness * (1.0 - threshold))
    inner = jnp.tanh(sharpness * (filtered - threshold))
    physical = (base + inner) / denominator
    steep = sharpness * (1.0 - inner * inner) / denominator
    return physical, steep


def ramp(physical):
    damping = damping_max * ramp_shape * (1.0 - physical) / (ramp_shape + physical)
    slope = -damping_max * ramp_shape * (1.0 + ramp_shape) / ((ramp_shape + physical) * (ramp_shape + physical))
    return damping, slope


def weighted_sum(members, factors):
    result = None
    for member, factor in zip(members, factors):
        if factor == 0:
            continue
        addend = factor * member
        result = addend if result is None else result + addend
    return result


def collide(pulled, forward, mask, damping, slope):
    forward_list = [forward[q] for q in range(Q)]
    density = weighted_sum(forward_list, [1.0] * Q)
    vel = [weighted_sum(forward_list, [float(d[a]) for d in velocity]) / density for a in range(3)]
    speed_sq = vel[0] * vel[0] + vel[1] * vel[1] + vel[2] * vel[2]
    zeroth = weighted_sum(pulled, lattice_weight)
    first = [weighted_sum(pulled, [w * d[a] for w, d in zip(lattice_weight, velocity)]) for a in range(3)]
    second = [[weighted_sum(pulled, [w * d[a] * d[b] for w, d in zip(lattice_weight, velocity)]) for b in range(3)] for a in range(3)]
    quadric = None
    for a in range(3):
        for b in range(3):
            addend = vel[a] * vel[b] * second[a][b]
            quadric = addend if quadric is None else quadric + addend
    eq_scalar = zeroth * (1.0 + 1.5 * speed_sq) - 4.5 * quadric
    eq_vector = [3.0 * first[a] + 9.0 * (second[a][0] * vel[0] + second[a][1] * vel[1] + second[a][2] * vel[2]) - 3.0 * zeroth * vel[a] for a in range(3)]
    moment = [weighted_sum(pulled, [float(d[a]) for d in velocity]) for a in range(3)]
    source = slope * (speed_sq - (vel[0] * moment[0] + vel[1] * moment[1] + vel[2] * moment[2]))
    outputs = []
    for q in range(Q):
        step_dir = velocity[q]
        along_eq = eq_scalar
        along_vel = 0.0
        for a in range(3):
            if step_dir[a] != 0:
                along_eq = along_eq + step_dir[a] * eq_vector[a]
                along_vel = along_vel + step_dir[a] * vel[a]
        own = pulled[q]
        fluid = (1.0 - relax_rate) * own + relax_rate * along_eq + 2.0 * damping * (along_vel - speed_sq) / density
        solid = pulled[opposite[q]]
        value = jnp.where(mask == 0, fluid, jnp.where(mask == 1, solid, jnp.where(mask == 2, along_eq, eq_scalar)))
        outputs.append(value)
    return jnp.stack(outputs), source


def reference(forward, adjoint, design, mask):
    filtered = smooth(design)
    physical, steep = project(filtered)
    damping, slope = ramp(physical)
    padded = jnp.pad(adjoint, ((0, 0), (1, 1), (1, 1), (1, 1)))
    extent = adjoint.shape[1:]
    pulled = []
    for q in range(Q):
        step_dir = velocity[q]
        begin = (1 + step_dir[0], 1 + step_dir[1], 1 + step_dir[2])
        pulled.append(lax.slice(padded[q], begin, (begin[0] + extent[0], begin[1] + extent[1], begin[2] + extent[2])))
    adjoint_next, source = collide(pulled, forward, mask, damping, slope)
    sensitivity = smooth(steep * source)
    return adjoint_next, sensitivity
```

```python
import functools
import math

import jax
import jax.numpy as jnp
from jax import lax
from jax.experimental import pallas as pl
from jax.experimental.pallas import tpu as pltpu
from jax.sharding import PartitionSpec as P

Q = 19
RADIUS = 8
MESH = pl.DeviceIdType.MESH
F32 = jnp.float32

velocity = [
    (0, 0, 0),
    (1, 0, 0),
    (-1, 0, 0),
    (0, 1, 0),
    (0, -1, 0),
    (0, 0, 1),
    (0, 0, -1),
    (1, 1, 0),
    (-1, -1, 0),
    (1, -1, 0),
    (-1, 1, 0),
    (1, 0, 1),
    (-1, 0, -1),
    (1, 0, -1),
    (-1, 0, 1),
    (0, 1, 1),
    (0, -1, -1),
    (0, 1, -1),
    (0, -1, 1),
]
lattice_weight = [1.0 / 3.0] + [1.0 / 18.0] * 6 + [1.0 / 36.0] * 12
opposite = [0, 2, 1, 4, 3, 6, 5, 8, 7, 10, 9, 12, 11, 14, 13, 16, 15, 18, 17]
relax_rate = 1.25
sharpness = 64.0
threshold = 0.5
damping_max = 10.0
ramp_shape = 0.1

slot_of = {5: 0, 6: 0, 11: 1, 12: 1, 14: 2, 13: 2, 15: 3, 16: 3, 18: 4, 17: 4}

unscaled = [math.exp(-(k * k) / (2.0 * (RADIUS / 2.0) ** 2)) for k in range(RADIUS + 1)]
tap_sum = unscaled[0] + 2.0 * sum(unscaled[1:])
TAPS = [v / tap_sum for v in unscaled]


def tap_matrix(offset):
    row = lax.broadcasted_iota(jnp.int32, (128, 128), 0)
    col = lax.broadcasted_iota(jnp.int32, (128, 128), 1)
    gap = jnp.abs(row + offset - col)
    result = jnp.zeros((128, 128), F32)
    for k in range(RADIUS + 1):
        result = jnp.where(gap == k, TAPS[k], result)
    return result


def symmetric(take):
    total = TAPS[0] * take(0)
    for k in range(1, RADIUS + 1):
        total = total + TAPS[k] * (take(k) + take(-k))
    return total


def filter_xy(source, middle, result):
    def along_x(group, carry):
        rows = pl.ds(pl.multiple_of(group * 8, 8), 8)
        planes = [source[i, rows, :] for i in range(32)]
        for i in range(16):
            middle[i, rows, :] = symmetric(lambda k: planes[i + 8 + k])
        return carry

    lax.fori_loop(0, 4, along_x, 0)

    def along_y(i, carry):
        for half in range(2):
            at = 8 + 8 * half
            result[i, pl.ds(8 * half, 8), :] = symmetric(
                lambda k: middle[i, pl.ds(at + k, 8), :]
            )
        return carry

    lax.fori_loop(0, 16, along_y, 0)


def dot(a, b):
    return jnp.dot(a, b, precision=lax.Precision.HIGHEST, preferred_element_type=F32)


def add_all(members):
    total = None
    for sign, member in members:
        if total is None:
            total = member if sign > 0 else -member
        else:
            total = total + member if sign > 0 else total - member
    return total


def main_kernel(
    forward,
    adjoint,
    design,
    mask,
    out,
    grad,
    padded,
    beside,
    flow,
    label,
    field,
    middle,
    smoothed,
    smoothed_beside,
    motion,
    chain,
    damp,
    raw,
    raw_beside,
    local_sem,
    send_sem,
    recv_sem,
):
    nx, ny = lax.axis_size("gx"), lax.axis_size("gy")
    X, Y, Z = lax.axis_index("gx"), lax.axis_index("gy"), lax.axis_index("gz")
    low_x, high_x = X > 0, X < nx - 1
    low_y, high_y = Y > 0, Y < ny - 1

    def exists(dx, dy):
        found = True
        if dx:
            found = high_x if dx > 0 else low_x
        if dy:
            found_y = high_y if dy > 0 else low_y
            found = found_y if found is True else jnp.logical_and(found, found_y)
        return found

    def when(cond, body):
        if cond is True:
            body()
        else:
            pl.when(cond)(body)

    def device(dx, dy, other):
        return (X + dx, Y + dy, 1 - Z if other else Z)

    loads = [
        pltpu.make_async_copy(design, field.at[8:24, 8:24, :], local_sem.at[0]),
        pltpu.make_async_copy(forward, flow, local_sem.at[1]),
        pltpu.make_async_copy(adjoint, padded.at[:, 1:17, 8:24, :], local_sem.at[2]),
        pltpu.make_async_copy(mask, label, local_sem.at[3]),
    ]
    for load in loads:
        load.start()

    around = [(dx, dy, 0) for dx in (-1, 0, 1) for dy in (-1, 0, 1) if dx or dy]
    around += [(0, 0, 1), (1, 0, 1), (-1, 0, 1), (0, 1, 1), (0, -1, 1)]
    barrier = pltpu.get_barrier_semaphore()
    for dx, dy, other in around:
        when(
            exists(dx, dy),
            lambda: pl.semaphore_signal(
                barrier, inc=1, device_id=device(dx, dy, other), device_id_type=MESH
            ),
        )

    plus_x = [q for q in range(Q) if velocity[q][0] > 0]
    minus_x = [q for q in range(Q) if velocity[q][0] < 0]
    plus_y = [q for q in range(Q) if velocity[q][1] > 0]
    minus_y = [q for q in range(Q) if velocity[q][1] < 0]

    def clear_x(side):
        plane = 0 if side < 0 else 17
        for q in minus_x if side < 0 else plus_x:
            padded[q, plane, :, :] = jnp.zeros((32, 128), F32)
        for slot in (1, 2):
            beside[slot, plane, :, :] = jnp.zeros((32, 128), F32)
        first = 0 if side < 0 else 24
        for ref in (field, grad):
            ref[first : first + 8, :, :] = jnp.zeros((8, 32, 128), F32)

    def clear_y(side):
        row = 7 if side < 0 else 24
        for q in minus_y if side < 0 else plus_y:
            for i in range(18):
                padded[q, i, row : row + 1, :] = jnp.zeros((1, 128), F32)
        for slot in (3, 4):
            for i in range(18):
                beside[slot, i, row : row + 1, :] = jnp.zeros((1, 128), F32)
        first = 0 if side < 0 else 24
        for ref in (field, grad):
            ref[:, first : first + 8, :] = jnp.zeros((32, 8, 128), F32)

    for side in (-1, 1):
        when(jnp.logical_not(exists(side, 0)), lambda: clear_x(side))
        when(jnp.logical_not(exists(0, side)), lambda: clear_y(side))

    sides_x = jnp.where(low_x, 1, 0) + jnp.where(high_x, 1, 0)
    sides_y = jnp.where(low_y, 1, 0) + jnp.where(high_y, 1, 0)
    pl.semaphore_wait(barrier, 1 + 2 * sides_x + 2 * sides_y + sides_x * sides_y)

    count = [0]

    def remote(src, dst, dx, dy, other, extra=None):
        copy = pltpu.make_async_remote_copy(
            src_ref=src,
            dst_ref=dst,
            send_sem=send_sem.at[count[0]],
            recv_sem=recv_sem.at[count[0]],
            device_id=device(dx, dy, other),
            device_id_type=MESH,
        )
        count[0] += 1
        return (exists(dx, dy), exists(-dx, -dy), copy, extra)

    def both(cond, extra):
        if extra is None:
            return cond
        return extra if cond is True else jnp.logical_and(cond, extra)

    def start(group):
        for sends, _, copy, extra in group:
            when(both(sends, extra and extra[0]), copy.start)

    def arrive(group):
        for _, receives, copy, extra in group:
            when(both(receives, extra and extra[1]), copy.wait_recv)

    def sent(group):
        for sends, _, copy, extra in group:
            when(both(sends, extra and extra[0]), copy.wait_send)

    def slab(ref, dx, dy):
        def own(d):
            return slice(8, 16) if d > 0 else slice(0, 8) if d < 0 else slice(0, 16)

        return ref.at[own(dx), own(dy), :]

    def halo(ref, dx, dy):
        def there(d):
            return slice(0, 8) if d > 0 else slice(24, 32) if d < 0 else slice(8, 24)

        return ref.at[there(dx), there(dy), :]

    order = [(1, 0), (-1, 0), (1, 1), (1, -1), (-1, 1), (-1, -1), (0, 1), (0, -1)]
    design_group = [
        remote(slab(design, dx, dy), halo(field, dx, dy), dx, dy, 0) for dx, dy in order
    ]
    start(design_group)

    faces = []
    for q in range(1, Q):
        cx, cy, cz = velocity[q]

        def pick(c, size):
            return slice(0, 1) if c > 0 else slice(size - 1, size) if c < 0 else slice(0, size)

        def put(c, low, size):
            return (
                slice(low + size, low + size + 1)
                if c > 0
                else slice(low - 1, low) if c < 0 else slice(low, low + size)
            )

        moves = []
        if cx:
            moves.append((cx, 0))
        if cy:
            moves.append((0, cy))
        if cx and cy:
            moves.append((cx, cy))
        for mx, my in moves:
            faces.append(
                remote(
                    adjoint.at[q, pick(mx, 16), pick(my, 16), :],
                    padded.at[q, put(mx, 1, 16), put(my, 8, 16), :],
                    -mx,
                    -my,
                    0,
                )
            )
            if cz:
                mine = Z == (1 if cz > 0 else 0)
                theirs = Z == (0 if cz > 0 else 1)
                faces.append(
                    remote(
                        adjoint.at[q, pick(mx, 16), pick(my, 16), :],
                        beside.at[slot_of[q], put(mx, 1, 16), put(my, 8, 16), :],
                        -mx,
                        -my,
                        1,
                        (mine, theirs),
                    )
                )
    start(faces)
    z_faces = []
    for q in (5, 11, 14, 15, 18):
        z_faces.append(
            remote(
                adjoint.at[q * Z + opposite[q] * (1 - Z)],
                beside.at[slot_of[q], 1:17, 8:24, :],
                0,
                0,
                1,
            )
        )
    start(z_faces)

    loads[1].wait()

    def flow_step(i, carry):
        for half in range(2):
            rows = pl.ds(8 * half, 8)
            f = [flow[q, i, rows, :] for q in range(Q)]
            scale = 1.0 / add_all([(1, f[q]) for q in range(Q)])
            vel = [
                add_all([(velocity[q][a], f[q]) for q in range(Q) if velocity[q][a]]) * scale
                for a in range(3)
            ]
            motion[0, i, rows, :] = scale
            for a in range(3):
                motion[1 + a, i, rows, :] = vel[a]
            motion[4, i, rows, :] = vel[0] * vel[0] + vel[1] * vel[1] + vel[2] * vel[2]
        return carry

    lax.fori_loop(0, 16, flow_step, 0)

    own_taps = tap_matrix(0)
    beside_taps = tap_matrix(jnp.where(Z == 0, 128, -128))

    loads[0].wait()
    arrive(design_group)
    filter_xy(field, middle, smoothed)
    swap = [remote(smoothed, smoothed_beside, 0, 0, 1)]
    start(swap)
    loads[2].wait()
    loads[3].wait()
    own_part = dot(smoothed[...].reshape(256, 128), own_taps)
    arrive(swap)
    filtered = own_part + dot(smoothed_beside[...].reshape(256, 128), beside_taps)
    base = math.tanh(sharpness * threshold)
    denominator = base + math.tanh(sharpness * (1.0 - threshold))
    inner = jnp.tanh(sharpness * (filtered - threshold))
    physical = (base + inner) / denominator
    steep = sharpness * (1.0 - inner * inner) / denominator
    inverse = 1.0 / (ramp_shape + physical)
    damp[...] = (damping_max * ramp_shape * (1.0 - physical) * inverse).reshape(16, 16, 128)
    chain[...] = (
        (-damping_max * ramp_shape * (1.0 + ramp_shape)) * steep * inverse * inverse
    ).reshape(16, 16, 128)

    arrive(faces)
    arrive(z_faces)

    lane = lax.broadcasted_iota(jnp.int32, (8, 128), 1)
    first, last = lane == 0, lane == 127
    first_open = lane == -Z
    last_open = lane == 128 * Z - 1

    def pulled_at(q, i, half):
        cx, cy, cz = velocity[q]
        rows = pl.ds(8 + 8 * half + cy, 8)
        own = padded[q, i + (1 + cx), rows, :]
        if cz == 0:
            return own
        edge = beside[slot_of[q], i + (1 + cx), rows, :]
        if cz > 0:
            joined = jnp.where(first, jnp.where(first_open, edge, 0.0), own)
            return pltpu.roll(joined, 127, 1)
        joined = jnp.where(last, jnp.where(last_open, edge, 0.0), own)
        return pltpu.roll(joined, 1, 1)

    def source_step(i, carry):
        for half in range(2):
            rows = pl.ds(8 * half, 8)
            p = [None] + [pulled_at(q, i, half) for q in range(1, Q)]
            moment = [
                add_all([(velocity[q][a], p[q]) for q in range(1, Q) if velocity[q][a]])
                for a in range(3)
            ]
            vel = [motion[1 + a, i, rows, :] for a in range(3)]
            along = vel[0] * moment[0] + vel[1] * moment[1] + vel[2] * moment[2]
            raw[i, rows, :] = chain[i, rows, :] * (motion[4, i, rows, :] - along)
        return carry

    lax.fori_loop(0, 16, source_step, 0)

    swap_raw = [remote(raw, raw_beside, 0, 0, 1)]
    start(swap_raw)
    own_grad = dot(raw[...].reshape(256, 128), own_taps)
    arrive(swap_raw)
    grad_z = own_grad + dot(raw_beside[...].reshape(256, 128), beside_taps)
    grad[8:24, 8:24, :] = grad_z.reshape(16, 16, 128)

    def own_slab(ref, dx, dy):
        def own(d):
            return slice(16, 24) if d > 0 else slice(8, 16) if d < 0 else slice(8, 24)

        return ref.at[own(dx), own(dy), :]

    grad_group = [
        remote(own_slab(grad, dx, dy), halo(grad, dx, dy), dx, dy, 0) for dx, dy in order
    ]
    start(grad_group)

    def collide_step(i, carry):
        for half in range(2):
            rows = pl.ds(8 * half, 8)
            p = [pulled_at(q, i, half) for q in range(Q)]
            scale = motion[0, i, rows, :]
            vel = [motion[1 + a, i, rows, :] for a in range(3)]
            speed_sq = motion[4, i, rows, :]
            damping = damp[i, rows, :]
            cell = label[i, rows, :]
            wp = [lattice_weight[q] * p[q] for q in range(Q)]
            zeroth = add_all([(1, wp[q]) for q in range(Q)])
            first_m = [
                add_all([(velocity[q][a], wp[q]) for q in range(Q) if velocity[q][a]])
                for a in range(3)
            ]
            second = {}
            for a in range(3):
                for b in range(a, 3):
                    second[a, b] = second[b, a] = add_all(
                        [
                            (velocity[q][a] * velocity[q][b], wp[q])
                            for q in range(Q)
                            if velocity[q][a] * velocity[q][b]
                        ]
                    )
            turned = [
                second[a, 0] * vel[0] + second[a, 1] * vel[1] + second[a, 2] * vel[2]
                for a in range(3)
            ]
            quadric = vel[0] * turned[0] + vel[1] * turned[1] + vel[2] * turned[2]
            eq_scalar = zeroth * (1.0 + 1.5 * speed_sq) - 4.5 * quadric
            eq_vector = [
                3.0 * first_m[a] + 9.0 * turned[a] - 3.0 * zeroth * vel[a] for a in range(3)
            ]
            drag = 2.0 * damping * scale
            fluid, solid, inlet = cell == 0, cell == 1, cell == 2
            for q in range(Q):
                c = velocity[q]
                parts = [(c[a], eq_vector[a]) for a in range(3) if c[a]]
                along_eq = add_all([(1, eq_scalar)] + parts) if parts else eq_scalar
                parts = [(c[a], vel[a]) for a in range(3) if c[a]]
                push = add_all(parts) - speed_sq if parts else -speed_sq
                moved = (1.0 - relax_rate) * p[q] + relax_rate * along_eq + drag * push
                value = jnp.where(
                    fluid,
                    moved,
                    jnp.where(solid, p[opposite[q]], jnp.where(inlet, along_eq, eq_scalar)),
                )
                out[q, i, rows, :] = value
        return carry

    lax.fori_loop(0, 16, collide_step, 0)

    arrive(grad_group)
    for group in (design_group, faces, z_faces, swap, swap_raw, grad_group):
        sent(group)


def final_kernel(next_in, grad, next_out, sensitivity, middle, result, sems):
    whole = pltpu.make_async_copy(next_in, next_out, sems.at[0])
    whole.start()
    filter_xy(grad, middle, result)
    last = pltpu.make_async_copy(result, sensitivity, sems.at[1])
    last.start()
    last.wait()
    whole.wait()


N_COPIES = 64


def local(forward, adjoint, design, mask):
    block = design.shape
    wide = (32, 32, 128)
    anywhere = pl.BlockSpec(memory_space=pl.ANY)
    in_vmem = pl.BlockSpec(memory_space=pltpu.VMEM)
    vmem = lambda shape, dtype=F32: pltpu.VMEM(shape, dtype)
    nxt, grad = pl.pallas_call(
        main_kernel,
        out_shape=(vmem((Q,) + block), vmem(wide)),
        in_specs=[anywhere] * 4,
        out_specs=(in_vmem, in_vmem),
        scratch_shapes=[
            vmem((Q, 18, 32, 128)),
            vmem((5, 18, 32, 128)),
            vmem((Q,) + block),
            vmem(block, jnp.int32),
            vmem(wide),
            vmem((16, 32, 128)),
            vmem(block),
            vmem(block),
            vmem((5,) + block),
            vmem(block),
            vmem(block),
            vmem(block),
            vmem(block),
            pltpu.SemaphoreType.DMA((4,)),
            pltpu.SemaphoreType.DMA((N_COPIES,)),
            pltpu.SemaphoreType.DMA((N_COPIES,)),
        ],
        compiler_params=pltpu.CompilerParams(collective_id=0, has_side_effects=True),
        name="adjoint_main",
    )(forward, adjoint, design, mask)
    keep = lambda a: pltpu.with_memory_space_constraint(a, pltpu.VMEM)
    return pl.pallas_call(
        final_kernel,
        out_shape=(
            jax.ShapeDtypeStruct((Q,) + block, F32),
            jax.ShapeDtypeStruct(block, F32),
        ),
        in_specs=[in_vmem, in_vmem],
        out_specs=(anywhere, anywhere),
        scratch_shapes=[
            vmem((16, 32, 128)),
            vmem(block),
            pltpu.SemaphoreType.DMA((2,)),
        ],
        name="adjoint_final",
    )(keep(nxt), keep(grad))


def solution(mesh):
    return jax.shard_map(
        local,
        mesh=mesh,
        in_specs=(
            P(None, "gx", "gy", "gz"),
            P(None, "gx", "gy", "gz"),
            P("gx", "gy", "gz"),
            P("gx", "gy", "gz"),
        ),
        out_specs=(P(None, "gx", "gy", "gz"), P("gx", "gy", "gz")),
        check_vma=False,
    )
```

```python
import functools
import math

import jax
import jax.numpy as jnp
from jax import lax
from jax.experimental import pallas as pl
from jax.experimental.pallas import tpu as pltpu
from jax.sharding import PartitionSpec as P

Q = 19
RADIUS = 8
MESH = pl.DeviceIdType.MESH
F32 = jnp.float32

velocity = [
    (0, 0, 0),
    (1, 0, 0),
    (-1, 0, 0),
    (0, 1, 0),
    (0, -1, 0),
    (0, 0, 1),
    (0, 0, -1),
    (1, 1, 0),
    (-1, -1, 0),
    (1, -1, 0),
    (-1, 1, 0),
    (1, 0, 1),
    (-1, 0, -1),
    (1, 0, -1),
    (-1, 0, 1),
    (0, 1, 1),
    (0, -1, -1),
    (0, 1, -1),
    (0, -1, 1),
]
lattice_weight = [1.0 / 3.0] + [1.0 / 18.0] * 6 + [1.0 / 36.0] * 12
opposite = [0, 2, 1, 4, 3, 6, 5, 8, 7, 10, 9, 12, 11, 14, 13, 16, 15, 18, 17]
relax_rate = 1.25
sharpness = 64.0
threshold = 0.5
damping_max = 10.0
ramp_shape = 0.1

slot_of = {5: 0, 6: 0, 11: 1, 12: 1, 14: 2, 13: 2, 15: 3, 16: 3, 18: 4, 17: 4}

unscaled = [math.exp(-(k * k) / (2.0 * (RADIUS / 2.0) ** 2)) for k in range(RADIUS + 1)]
tap_sum = unscaled[0] + 2.0 * sum(unscaled[1:])
TAPS = [v / tap_sum for v in unscaled]


def tap_matrix(offset):
    row = lax.broadcasted_iota(jnp.int32, (128, 128), 0)
    col = lax.broadcasted_iota(jnp.int32, (128, 128), 1)
    gap = jnp.abs(row + offset - col)
    result = jnp.zeros((128, 128), F32)
    for k in range(RADIUS + 1):
        result = jnp.where(gap == k, TAPS[k], result)
    return result


def symmetric(take):
    total = TAPS[0] * take(0)
    for k in range(1, RADIUS + 1):
        total = total + TAPS[k] * (take(k) + take(-k))
    return total


def filter_xy(source, middle, result):
    def along_x(group, carry):
        rows = pl.ds(pl.multiple_of(group * 8, 8), 8)
        planes = [source[i, rows, :] for i in range(32)]
        for i in range(16):
            middle[i, rows, :] = symmetric(lambda k: planes[i + 8 + k])
        return carry

    lax.fori_loop(0, 4, along_x, 0)

    def along_y(i, carry):
        for half in range(2):
            at = 8 + 8 * half
            result[i, pl.ds(8 * half, 8), :] = symmetric(
                lambda k: middle[i, pl.ds(at + k, 8), :]
            )
        return carry

    lax.fori_loop(0, 16, along_y, 0)


def dot(a, b):
    return jnp.dot(a, b, precision=lax.Precision.HIGHEST, preferred_element_type=F32)


def add_all(members):
    total = None
    for sign, member in members:
        if total is None:
            total = member if sign > 0 else -member
        else:
            total = total + member if sign > 0 else total - member
    return total


def main_kernel(
    forward,
    adjoint,
    design,
    mask,
    out,
    grad,
    padded,
    beside,
    face_x,
    face_y,
    halo_x,
    halo_y,
    flow,
    label,
    field,
    middle,
    smoothed,
    smoothed_beside,
    motion,
    chain,
    damp,
    raw,
    raw_beside,
    local_sem,
    send_sem,
    recv_sem,
):
    nx, ny = lax.axis_size("gx"), lax.axis_size("gy")
    X, Y, Z = lax.axis_index("gx"), lax.axis_index("gy"), lax.axis_index("gz")
    low_x, high_x = X > 0, X < nx - 1
    low_y, high_y = Y > 0, Y < ny - 1

    def exists(dx, dy):
        found = True
        if dx:
            found = high_x if dx > 0 else low_x
        if dy:
            found_y = high_y if dy > 0 else low_y
            found = found_y if found is True else jnp.logical_and(found, found_y)
        return found

    def when(cond, body):
        if cond is True:
            body()
        else:
            pl.when(cond)(body)

    def device(dx, dy, other):
        return (X + dx, Y + dy, 1 - Z if other else Z)

    loads = [
        pltpu.make_async_copy(design, field.at[8:24, 8:24, :], local_sem.at[0]),
        pltpu.make_async_copy(forward, flow, local_sem.at[1]),
        pltpu.make_async_copy(adjoint, padded.at[:, 1:17, 8:24, :], local_sem.at[2]),
        pltpu.make_async_copy(mask, label, local_sem.at[3]),
    ]
    for load in loads:
        load.start()

    around = [(dx, dy, 0) for dx in (-1, 0, 1) for dy in (-1, 0, 1) if dx or dy]
    around.append((0, 0, 1))
    barrier = pltpu.get_barrier_semaphore()
    for dx, dy, other in around:
        when(
            exists(dx, dy),
            lambda: pl.semaphore_signal(
                barrier, inc=1, device_id=device(dx, dy, other), device_id_type=MESH
            ),
        )

    plus_x = [q for q in range(Q) if velocity[q][0] > 0]
    minus_x = [q for q in range(Q) if velocity[q][0] < 0]
    plus_y = [q for q in range(Q) if velocity[q][1] > 0]
    minus_y = [q for q in range(Q) if velocity[q][1] < 0]

    def clear_x(side):
        plane = 0 if side < 0 else 17
        for q in minus_x if side < 0 else plus_x:
            padded[q, plane, :, :] = jnp.zeros((32, 128), F32)
        first = 0 if side < 0 else 24
        for ref in (field, grad):
            ref[first : first + 8, :, :] = jnp.zeros((8, 32, 128), F32)

    def clear_y(side):
        row = 7 if side < 0 else 24
        for q in minus_y if side < 0 else plus_y:
            for i in range(18):
                padded[q, i, row : row + 1, :] = jnp.zeros((1, 128), F32)
        first = 0 if side < 0 else 24
        for ref in (field, grad):
            ref[:, first : first + 8, :] = jnp.zeros((32, 8, 128), F32)

    for side in (-1, 1):
        when(jnp.logical_not(exists(side, 0)), lambda: clear_x(side))
        when(jnp.logical_not(exists(0, side)), lambda: clear_y(side))

    sides_x = jnp.where(low_x, 1, 0) + jnp.where(high_x, 1, 0)
    sides_y = jnp.where(low_y, 1, 0) + jnp.where(high_y, 1, 0)
    pl.semaphore_wait(barrier, 1 + sides_x + sides_y + sides_x * sides_y)

    count = [0]

    def remote(src, dst, dx, dy, other, extra=None):
        copy = pltpu.make_async_remote_copy(
            src_ref=src,
            dst_ref=dst,
            send_sem=send_sem.at[count[0]],
            recv_sem=recv_sem.at[count[0]],
            device_id=device(dx, dy, other),
            device_id_type=MESH,
        )
        count[0] += 1
        return (exists(dx, dy), exists(-dx, -dy), copy, extra)

    def both(cond, extra):
        if extra is None:
            return cond
        return extra if cond is True else jnp.logical_and(cond, extra)

    def start(group):
        for sends, _, copy, extra in group:
            when(both(sends, extra and extra[0]), copy.start)

    def arrive(group):
        for _, receives, copy, extra in group:
            when(both(receives, extra and extra[1]), copy.wait_recv)

    def sent(group):
        for sends, _, copy, extra in group:
            when(both(sends, extra and extra[0]), copy.wait_send)

    def slab(ref, dx, dy):
        def own(d):
            return slice(8, 16) if d > 0 else slice(0, 8) if d < 0 else slice(0, 16)

        return ref.at[own(dx), own(dy), :]

    def halo(ref, dx, dy):
        def there(d):
            return slice(0, 8) if d > 0 else slice(24, 32) if d < 0 else slice(8, 24)

        return ref.at[there(dx), there(dy), :]

    order = [(1, 0), (-1, 0), (1, 1), (1, -1), (-1, 1), (-1, -1), (0, 1), (0, -1)]
    design_group = [
        remote(slab(design, dx, dy), halo(field, dx, dy), dx, dy, 0) for dx, dy in order
    ]
    start(design_group)

    z_faces = [
        remote(adjoint.at[q * Z + opposite[q] * (1 - Z)], beside.at[slot_of[q]], 0, 0, 1)
        for q in (5, 11, 14, 15, 18)
    ]
    start(z_faces)

    loads[1].wait()

    def flow_step(i, carry):
        for half in range(2):
            rows = pl.ds(8 * half, 8)
            f = [flow[q, i, rows, :] for q in range(Q)]
            scale = 1.0 / add_all([(1, f[q]) for q in range(Q)])
            vel = [
                add_all([(velocity[q][a], f[q]) for q in range(Q) if velocity[q][a]]) * scale
                for a in range(3)
            ]
            motion[0, i, rows, :] = scale
            for a in range(3):
                motion[1 + a, i, rows, :] = vel[a]
            motion[4, i, rows, :] = vel[0] * vel[0] + vel[1] * vel[1] + vel[2] * vel[2]
        return carry

    lax.fori_loop(0, 16, flow_step, 0)

    own_taps = tap_matrix(0)
    beside_taps = tap_matrix(jnp.where(Z == 0, 128, -128))

    lane = lax.broadcasted_iota(jnp.int32, (16, 128), 1)
    first, last = lane == 0, lane == 127
    first_open = lane == -Z
    last_open = lane == 128 * Z - 1
    loads[2].wait()
    arrive(z_faces)

    def pull_z(i, carry):
        for q in slot_of:
            own = padded[q, i + 1, 8:24, :]
            edge = beside[slot_of[q], i, :, :]
            if velocity[q][2] > 0:
                joined = jnp.where(first, jnp.where(first_open, edge, 0.0), own)
                shifted = pltpu.roll(joined, 127, 1)
            else:
                joined = jnp.where(last, jnp.where(last_open, edge, 0.0), own)
                shifted = pltpu.roll(joined, 1, 1)
            padded[q, i + 1, 8:24, :] = shifted
        return carry

    lax.fori_loop(0, 16, pull_z, 0)
    for k in range(5):
        face_x[0, k, :, :] = padded[minus_x[k], 16, 8:24, :]
        face_x[1, k, :, :] = padded[plus_x[k], 1, 8:24, :]
        face_y[0, k, :, :] = padded[minus_y[k], 1:17, 23, :]
        face_y[1, k, :, :] = padded[plus_y[k], 1:17, 8, :]
    faces = [
        remote(face_x.at[0], halo_x.at[0], 1, 0, 0),
        remote(face_x.at[1], halo_x.at[1], -1, 0, 0),
        remote(face_y.at[0], halo_y.at[0], 0, 1, 0),
        remote(face_y.at[1], halo_y.at[1], 0, -1, 0),
    ]
    for q in (7, 8, 9, 10):
        cx, cy, cz = velocity[q]
        faces.append(
            remote(
                adjoint.at[q, slice(0, 1) if cx > 0 else slice(15, 16), slice(0, 1) if cy > 0 else slice(15, 16), :],
                padded.at[q, slice(17, 18) if cx > 0 else slice(0, 1), slice(24, 25) if cy > 0 else slice(7, 8), :],
                -cx,
                -cy,
                0,
            )
        )
    start(faces)

    loads[0].wait()
    arrive(design_group)
    filter_xy(field, middle, smoothed)
    swap = [remote(smoothed, smoothed_beside, 0, 0, 1)]
    start(swap)
    loads[3].wait()
    own_part = dot(smoothed[...].reshape(256, 128), own_taps)
    arrive(swap)
    filtered = own_part + dot(smoothed_beside[...].reshape(256, 128), beside_taps)
    base = math.tanh(sharpness * threshold)
    denominator = base + math.tanh(sharpness * (1.0 - threshold))
    inner = jnp.tanh(sharpness * (filtered - threshold))
    physical = (base + inner) / denominator
    steep = sharpness * (1.0 - inner * inner) / denominator
    inverse = 1.0 / (ramp_shape + physical)
    damp[...] = (damping_max * ramp_shape * (1.0 - physical) * inverse).reshape(16, 16, 128)
    chain[...] = (
        (-damping_max * ramp_shape * (1.0 + ramp_shape)) * steep * inverse * inverse
    ).reshape(16, 16, 128)

    arrive(faces)

    def place_x(side):
        for k in range(5):
            q, plane = ((plus_x if side else minus_x)[k], 17 if side else 0)
            padded[q, plane, 8:24, :] = halo_x[side, k, :, :]

    def place_y(side):
        for k in range(5):
            q, row = ((plus_y if side else minus_y)[k], 24 if side else 7)
            padded[q, 1:17, row, :] = halo_y[side, k, :, :]

    for side in (0, 1):
        when(exists(2 * side - 1, 0), lambda: place_x(side))
        when(exists(0, 2 * side - 1), lambda: place_y(side))

    def pulled_at(q, i, half):
        cx, cy, cz = velocity[q]
        return padded[q, i + (1 + cx), pl.ds(8 + 8 * half + cy, 8), :]

    def source_step(i, carry):
        for half in range(2):
            rows = pl.ds(8 * half, 8)
            p = [None] + [pulled_at(q, i, half) for q in range(1, Q)]
            moment = [
                add_all([(velocity[q][a], p[q]) for q in range(1, Q) if velocity[q][a]])
                for a in range(3)
            ]
            vel = [motion[1 + a, i, rows, :] for a in range(3)]
            along = vel[0] * moment[0] + vel[1] * moment[1] + vel[2] * moment[2]
            raw[i, rows, :] = chain[i, rows, :] * (motion[4, i, rows, :] - along)
        return carry

    lax.fori_loop(0, 16, source_step, 0)

    swap_raw = [remote(raw, raw_beside, 0, 0, 1)]
    start(swap_raw)
    own_grad = dot(raw[...].reshape(256, 128), own_taps)
    arrive(swap_raw)
    grad_z = own_grad + dot(raw_beside[...].reshape(256, 128), beside_taps)
    grad[8:24, 8:24, :] = grad_z.reshape(16, 16, 128)

    def own_slab(ref, dx, dy):
        def own(d):
            return slice(16, 24) if d > 0 else slice(8, 16) if d < 0 else slice(8, 24)

        return ref.at[own(dx), own(dy), :]

    grad_group = [
        remote(own_slab(grad, dx, dy), halo(grad, dx, dy), dx, dy, 0) for dx, dy in order
    ]
    start(grad_group)

    def collide_step(i, carry):
        for half in range(2):
            rows = pl.ds(8 * half, 8)
            p = [pulled_at(q, i, half) for q in range(Q)]
            scale = motion[0, i, rows, :]
            vel = [motion[1 + a, i, rows, :] for a in range(3)]
            speed_sq = motion[4, i, rows, :]
            damping = damp[i, rows, :]
            cell = label[i, rows, :]
            wp = [lattice_weight[q] * p[q] for q in range(Q)]
            zeroth = add_all([(1, wp[q]) for q in range(Q)])
            first_m = [
                add_all([(velocity[q][a], wp[q]) for q in range(Q) if velocity[q][a]])
                for a in range(3)
            ]
            second = {}
            for a in range(3):
                for b in range(a, 3):
                    second[a, b] = second[b, a] = add_all(
                        [
                            (velocity[q][a] * velocity[q][b], wp[q])
                            for q in range(Q)
                            if velocity[q][a] * velocity[q][b]
                        ]
                    )
            turned = [
                second[a, 0] * vel[0] + second[a, 1] * vel[1] + second[a, 2] * vel[2]
                for a in range(3)
            ]
            quadric = vel[0] * turned[0] + vel[1] * turned[1] + vel[2] * turned[2]
            eq_scalar = zeroth * (1.0 + 1.5 * speed_sq) - 4.5 * quadric
            eq_vector = [
                3.0 * first_m[a] + 9.0 * turned[a] - 3.0 * zeroth * vel[a] for a in range(3)
            ]
            drag = 2.0 * damping * scale
            fluid, solid, inlet = cell == 0, cell == 1, cell == 2
            for q in range(Q):
                c = velocity[q]
                parts = [(c[a], eq_vector[a]) for a in range(3) if c[a]]
                along_eq = add_all([(1, eq_scalar)] + parts) if parts else eq_scalar
                parts = [(c[a], vel[a]) for a in range(3) if c[a]]
                push = add_all(parts) - speed_sq if parts else -speed_sq
                moved = (1.0 - relax_rate) * p[q] + relax_rate * along_eq + drag * push
                value = jnp.where(
                    fluid,
                    moved,
                    jnp.where(solid, p[opposite[q]], jnp.where(inlet, along_eq, eq_scalar)),
                )
                out[q, i, rows, :] = value
        return carry

    lax.fori_loop(0, 16, collide_step, 0)

    arrive(grad_group)
    for group in (design_group, faces, z_faces, swap, swap_raw, grad_group):
        sent(group)


def final_kernel(next_in, grad, next_out, sensitivity, middle, result, sems):
    whole = pltpu.make_async_copy(next_in, next_out, sems.at[0])
    whole.start()
    filter_xy(grad, middle, result)
    last = pltpu.make_async_copy(result, sensitivity, sems.at[1])
    last.start()
    last.wait()
    whole.wait()


N_COPIES = 64


def local(forward, adjoint, design, mask):
    block = design.shape
    wide = (32, 32, 128)
    anywhere = pl.BlockSpec(memory_space=pl.ANY)
    in_vmem = pl.BlockSpec(memory_space=pltpu.VMEM)
    vmem = lambda shape, dtype=F32: pltpu.VMEM(shape, dtype)
    nxt, grad = pl.pallas_call(
        main_kernel,
        out_shape=(vmem((Q,) + block), vmem(wide)),
        in_specs=[anywhere] * 4,
        out_specs=(in_vmem, in_vmem),
        scratch_shapes=[
            vmem((Q, 18, 32, 128)),
            vmem((5,) + block),
            vmem((2, 5, 16, 128)),
            vmem((2, 5, 16, 128)),
            vmem((2, 5, 16, 128)),
            vmem((2, 5, 16, 128)),
            vmem((Q,) + block),
            vmem(block, jnp.int32),
            vmem(wide),
            vmem((16, 32, 128)),
            vmem(block),
            vmem(block),
            vmem((5,) + block),
            vmem(block),
            vmem(block),
            vmem(block),
            vmem(block),
            pltpu.SemaphoreType.DMA((4,)),
            pltpu.SemaphoreType.DMA((N_COPIES,)),
            pltpu.SemaphoreType.DMA((N_COPIES,)),
        ],
        compiler_params=pltpu.CompilerParams(collective_id=0, has_side_effects=True),
        name="adjoint_main",
    )(forward, adjoint, design, mask)
    keep = lambda a: pltpu.with_memory_space_constraint(a, pltpu.VMEM)
    return pl.pallas_call(
        final_kernel,
        out_shape=(
            jax.ShapeDtypeStruct((Q,) + block, F32),
            jax.ShapeDtypeStruct(block, F32),
        ),
        in_specs=[in_vmem, in_vmem],
        out_specs=(anywhere, anywhere),
        scratch_shapes=[
            vmem((16, 32, 128)),
            vmem(block),
            pltpu.SemaphoreType.DMA((2,)),
        ],
        name="adjoint_final",
    )(keep(nxt), keep(grad))


def solution(mesh):
    return jax.shard_map(
        local,
        mesh=mesh,
        in_specs=(
            P(None, "gx", "gy", "gz"),
            P(None, "gx", "gy", "gz"),
            P("gx", "gy", "gz"),
            P("gx", "gy", "gz"),
        ),
        out_specs=(P(None, "gx", "gy", "gz"), P("gx", "gy", "gz")),
        check_vma=False,
    )
```

```python
import functools
import math

import jax
import jax.numpy as jnp
from jax import lax
from jax.experimental import pallas as pl
from jax.experimental.pallas import tpu as pltpu
from jax.sharding import PartitionSpec as P

Q = 19
RADIUS = 8
MESH = pl.DeviceIdType.MESH
F32 = jnp.float32

velocity = [
    (0, 0, 0),
    (1, 0, 0),
    (-1, 0, 0),
    (0, 1, 0),
    (0, -1, 0),
    (0, 0, 1),
    (0, 0, -1),
    (1, 1, 0),
    (-1, -1, 0),
    (1, -1, 0),
    (-1, 1, 0),
    (1, 0, 1),
    (-1, 0, -1),
    (1, 0, -1),
    (-1, 0, 1),
    (0, 1, 1),
    (0, -1, -1),
    (0, 1, -1),
    (0, -1, 1),
]
lattice_weight = [1.0 / 3.0] + [1.0 / 18.0] * 6 + [1.0 / 36.0] * 12
opposite = [0, 2, 1, 4, 3, 6, 5, 8, 7, 10, 9, 12, 11, 14, 13, 16, 15, 18, 17]
relax_rate = 1.25
sharpness = 64.0
threshold = 0.5
damping_max = 10.0
ramp_shape = 0.1

slot_of = {5: 0, 6: 0, 11: 1, 12: 1, 14: 2, 13: 2, 15: 3, 16: 3, 18: 4, 17: 4}

unscaled = [math.exp(-(k * k) / (2.0 * (RADIUS / 2.0) ** 2)) for k in range(RADIUS + 1)]
tap_sum = unscaled[0] + 2.0 * sum(unscaled[1:])
TAPS = [v / tap_sum for v in unscaled]


def tap_matrix(offset):
    row = lax.broadcasted_iota(jnp.int32, (128, 128), 0)
    col = lax.broadcasted_iota(jnp.int32, (128, 128), 1)
    gap = jnp.abs(row + offset - col)
    result = jnp.zeros((128, 128), F32)
    for k in range(RADIUS + 1):
        result = jnp.where(gap == k, TAPS[k], result)
    return result


def symmetric(take):
    total = TAPS[0] * take(0)
    for k in range(1, RADIUS + 1):
        total = total + TAPS[k] * (take(k) + take(-k))
    return total


def filter_xy(source, edges, middle, result):
    Z = lax.axis_index("gz")
    lane = lax.broadcasted_iota(jnp.int32, (8, 128), 1)
    lowest = 120 * (1 - Z)
    edge = jnp.logical_and(lane >= lowest, lane < lowest + 8)

    def spread(n, u):
        whole_row = edges[n, :, :]
        if u:
            whole_row = pltpu.roll(whole_row, 128 - 8 * u, 1)
        return jnp.where(edge, whole_row, 0.0)

    for group in range(4):
        rows = slice(8 * group, 8 * group + 8)
        dy = 1 if group == 0 else -1 if group == 3 else 0
        planes = []
        for i in range(32):
            plane = source[i, rows, :]
            dx = 1 if i < 8 else -1 if i >= 24 else 0
            if dx or dy:
                if dx == 0:
                    u = i - 8
                else:
                    u = 2 * (i % 8) + (group - 1 if dy == 0 else 1 if dy > 0 else 0)
                plane = plane + spread(ORDER.index((dx, dy)), u)
            planes.append(plane)
        for i in range(16):
            middle[i, rows, :] = symmetric(lambda k: planes[i + 8 + k])
    filter_y(middle, result)


def filter_y(middle, result):
    def along_y(i, carry):
        rows = [middle[i, pl.ds(at, 8), :] for at in range(25)]
        for half in range(2):
            result[i, pl.ds(8 * half, 8), :] = symmetric(lambda k: rows[8 + 8 * half + k])
        return carry

    lax.fori_loop(0, 16, along_y, 0)


ORDER = [(1, 0), (-1, 0), (1, 1), (1, -1), (-1, 1), (-1, -1), (0, 1), (0, -1)]


def packed(units):
    total = units[0]
    for u in range(1, 16):
        total = total + pltpu.roll(units[u], 8 * u, 1)
    return total


def dot(a, b):
    return jnp.dot(a, b, precision=lax.Precision.HIGHEST, preferred_element_type=F32)


def add_all(members):
    total = None
    for sign, member in members:
        if total is None:
            total = member if sign > 0 else -member
        else:
            total = total + member if sign > 0 else total - member
    return total


def main_kernel(
    forward,
    adjoint,
    design,
    mask,
    out,
    grad,
    edges,
    padded,
    beside,
    face_x,
    face_y,
    halo_x,
    halo_y,
    flow,
    label,
    plain,
    own_design,
    design_beside,
    field,
    field_out,
    field_edges,
    middle,
    smoothed,
    motion,
    chain,
    damp,
    raw,
    raw_beside,
    lean,
    own_side,
    edge_out,
    local_sem,
    send_sem,
    recv_sem,
):
    nx, ny = lax.axis_size("gx"), lax.axis_size("gy")
    X, Y, Z = lax.axis_index("gx"), lax.axis_index("gy"), lax.axis_index("gz")
    low_x, high_x = X > 0, X < nx - 1
    low_y, high_y = Y > 0, Y < ny - 1

    def exists(dx, dy):
        found = True
        if dx:
            found = high_x if dx > 0 else low_x
        if dy:
            found_y = high_y if dy > 0 else low_y
            found = found_y if found is True else jnp.logical_and(found, found_y)
        return found

    def when(cond, body):
        if cond is True:
            body()
        else:
            pl.when(cond)(body)

    def device(dx, dy, other):
        return (X + dx, Y + dy, 1 - Z if other else Z)

    loads = [
        pltpu.make_async_copy(design, plain, local_sem.at[0]),
        pltpu.make_async_copy(forward, flow, local_sem.at[1]),
        pltpu.make_async_copy(adjoint, padded.at[:, 1:17, 8:24, :], local_sem.at[2]),
        pltpu.make_async_copy(mask, label, local_sem.at[3]),
    ]
    for load in loads:
        load.start()

    around = [(dx, dy, 0) for dx in (-1, 0, 1) for dy in (-1, 0, 1) if dx or dy]
    around.append((0, 0, 1))
    barrier = pltpu.get_barrier_semaphore()
    for dx, dy, other in around:
        when(
            exists(dx, dy),
            lambda: pl.semaphore_signal(
                barrier, inc=1, device_id=device(dx, dy, other), device_id_type=MESH
            ),
        )

    plus_x = [q for q in range(Q) if velocity[q][0] > 0]
    minus_x = [q for q in range(Q) if velocity[q][0] < 0]
    plus_y = [q for q in range(Q) if velocity[q][1] > 0]
    minus_y = [q for q in range(Q) if velocity[q][1] < 0]

    for q in minus_x + plus_x:
        padded[q, 17 if q in plus_x else 0, :, :] = jnp.zeros((32, 128), F32)
    for q in minus_y + plus_y:
        padded[q, 1:17, 24 if q in plus_y else 7, :] = jnp.zeros((16, 128), F32)
    for side in range(2):
        for k in range(5):
            for row in (7, 24):
                halo_y[side, k, row : row + 1, :] = jnp.zeros((1, 128), F32)

    def clear_x(side):
        halo_x[max(side, 0), :, 8:24, :] = jnp.zeros((5, 16, 128), F32)
        begin = 0 if side < 0 else 24
        for ref in (field, grad):
            ref[begin : begin + 8, :, :] = jnp.zeros((8, 32, 128), F32)

    def clear_y(side):
        halo_y[max(side, 0), :, 8:24, :] = jnp.zeros((5, 16, 128), F32)
        begin = 0 if side < 0 else 24
        for ref in (field, grad):
            ref[:, begin : begin + 8, :] = jnp.zeros((32, 8, 128), F32)

    def corner(q):
        cx, cy, cz = velocity[q]
        k = (plus_x if cx > 0 else minus_x).index(q)
        return (1 if cx > 0 else 0), k, slice(24, 25) if cy > 0 else slice(7, 8)

    def clear_corner(q):
        side, k, row = corner(q)
        halo_x[side, k, row, :] = jnp.zeros((1, 128), F32)

    def clear_edge(n):
        for ref in (edges, field_edges):
            ref[n, :, :] = jnp.zeros((8, 128), F32)

    for n, (dx, dy) in enumerate(ORDER):
        when(jnp.logical_not(exists(-dx, -dy)), lambda: clear_edge(n))
    for q in (7, 8, 9, 10):
        cx, cy, cz = velocity[q]
        when(jnp.logical_not(exists(cx, cy)), lambda: clear_corner(q))
    for side in (-1, 1):
        when(jnp.logical_not(exists(side, 0)), lambda: clear_x(side))
        when(jnp.logical_not(exists(0, side)), lambda: clear_y(side))

    own_taps = tap_matrix(0)
    beside_taps = tap_matrix(jnp.where(Z == 0, 128, -128))
    loads[0].wait()
    own_design[...] = dot(plain[...].reshape(256, 128), own_taps).reshape(16, 16, 128)
    sides_x = jnp.where(low_x, 1, 0) + jnp.where(high_x, 1, 0)
    sides_y = jnp.where(low_y, 1, 0) + jnp.where(high_y, 1, 0)
    pl.semaphore_wait(barrier, 1 + sides_x + sides_y + sides_x * sides_y)

    count = [0]

    def remote(src, dst, dx, dy, other, extra=None):
        copy = pltpu.make_async_remote_copy(
            src_ref=src,
            dst_ref=dst,
            send_sem=send_sem.at[count[0]],
            recv_sem=recv_sem.at[count[0]],
            device_id=device(dx, dy, other),
            device_id_type=MESH,
        )
        count[0] += 1
        return (exists(dx, dy), exists(-dx, -dy), copy, extra)

    def both(cond, extra):
        if extra is None:
            return cond
        return extra if cond is True else jnp.logical_and(cond, extra)

    def start(group):
        for sends, _, copy, extra in group:
            when(both(sends, extra and extra[0]), copy.start)

    def arrive(group):
        for _, receives, copy, extra in group:
            when(both(receives, extra and extra[1]), copy.wait_recv)

    def sent(group):
        for sends, _, copy, extra in group:
            when(both(sends, extra and extra[0]), copy.wait_send)

    def slab(ref, dx, dy):
        def own(d):
            return slice(8, 16) if d > 0 else slice(0, 8) if d < 0 else slice(0, 16)

        return ref.at[own(dx), own(dy), :]

    def halo(ref, dx, dy):
        def there(d):
            return slice(0, 8) if d > 0 else slice(24, 32) if d < 0 else slice(8, 24)

        return ref.at[there(dx), there(dy), :]

    def slabs(own, result):
        return [remote(slab(own, dx, dy), halo(result, dx, dy), dx, dy, 0) for dx, dy in ORDER]

    def join(own, received, result, packs, landing):
        other = dot(received[...].reshape(256, 128), beside_taps).reshape(16, 16, 128)
        result[8:24, 8:24, :] = own[...] + other
        for side in range(2):
            at = 0 if side else 8
            packs[side, :, :] = packed(
                [other[at + p, 8 * g : 8 * g + 8, :] for p in range(8) for g in range(2)]
            )
            packs[2 + side, :, :] = packed([other[i, at : at + 8, :] for i in range(16)])
        return [
            remote(
                packs.at[(0 if dx > 0 else 1) if dx else (2 if dy > 0 else 3)],
                landing.at[n],
                dx,
                dy,
                0,
            )
            for n, (dx, dy) in enumerate(ORDER)
        ]

    swap = [remote(design, design_beside, 0, 0, 1)]
    design_group = slabs(own_design, field)
    start(swap)
    start(design_group)

    z_faces = [
        remote(adjoint.at[q * Z + opposite[q] * (1 - Z)], beside.at[slot_of[q]], 0, 0, 1)
        for q in (5, 11, 14, 15, 18)
    ]
    start(z_faces)

    arrive(swap)
    field_group = join(own_design, design_beside, field, field_out, field_edges)
    start(field_group)

    lane = lax.broadcasted_iota(jnp.int32, (16, 128), 1)
    first, last = lane == 0, lane == 127
    first_open = lane == -Z
    last_open = lane == 128 * Z - 1
    loads[2].wait()
    arrive(z_faces)

    def pull_z(i, carry):
        for q in slot_of:
            own = padded[q, i + 1, 8:24, :]
            edge = beside[slot_of[q], i, :, :]
            if velocity[q][2] > 0:
                joined = jnp.where(first, jnp.where(first_open, edge, 0.0), own)
                shifted = pltpu.roll(joined, 127, 1)
            else:
                joined = jnp.where(last, jnp.where(last_open, edge, 0.0), own)
                shifted = pltpu.roll(joined, 1, 1)
            padded[q, i + 1, 8:24, :] = shifted
        return carry

    lax.fori_loop(0, 16, pull_z, 0)
    for k in range(5):
        face_x[0, k, :, :] = padded[minus_x[k], 16, 8:24, :]
        face_x[1, k, :, :] = padded[plus_x[k], 1, 8:24, :]
        face_y[0, k, :, :] = padded[minus_y[k], 1:17, 23, :]
        face_y[1, k, :, :] = padded[plus_y[k], 1:17, 8, :]
    faces = [
        remote(face_x.at[0], halo_x.at[0, :, 8:24, :], 1, 0, 0),
        remote(face_x.at[1], halo_x.at[1, :, 8:24, :], -1, 0, 0),
        remote(face_y.at[0], halo_y.at[0, :, 8:24, :], 0, 1, 0),
        remote(face_y.at[1], halo_y.at[1, :, 8:24, :], 0, -1, 0),
    ]
    for q in (7, 8, 9, 10):
        cx, cy, cz = velocity[q]
        side, k, row = corner(q)
        faces.append(
            remote(
                adjoint.at[q, 0 if cx > 0 else 15, slice(0, 1) if cy > 0 else slice(15, 16), :],
                halo_x.at[side, k, row, :],
                -cx,
                -cy,
                0,
            )
        )
    start(faces)

    loads[1].wait()

    def flow_step(i, carry):
        for half in range(2):
            rows = pl.ds(8 * half, 8)
            f = [flow[q, i, rows, :] for q in range(Q)]
            scale = 1.0 / add_all([(1, f[q]) for q in range(Q)])
            vel = [
                add_all([(velocity[q][a], f[q]) for q in range(Q) if velocity[q][a]]) * scale
                for a in range(3)
            ]
            motion[0, i, rows, :] = scale
            for a in range(3):
                motion[1 + a, i, rows, :] = vel[a]
            motion[4, i, rows, :] = vel[0] * vel[0] + vel[1] * vel[1] + vel[2] * vel[2]
        return carry

    lax.fori_loop(0, 16, flow_step, 0)


    def pulled_at(q, i, half):
        cx, cy, cz = velocity[q]
        return padded[q, i + (1 + cx), pl.ds(8 + 8 * half + cy, 8), :]

    def moment_step(i, carry):
        for half in range(2):
            rows = pl.ds(8 * half, 8)
            p = [None] + [pulled_at(q, i, half) for q in range(1, Q)]
            total = motion[4, i, rows, :]
            for axis in range(3):
                moment = add_all([(velocity[q][axis], p[q]) for q in range(1, Q) if velocity[q][axis]])
                total = total - motion[1 + axis, i, rows, :] * moment
            lean[i, rows, :] = total
        return carry

    lax.fori_loop(0, 16, moment_step, 0)
    arrive(design_group)
    arrive(field_group)
    filter_xy(field, field_edges, middle, smoothed)
    loads[3].wait()
    filtered = smoothed[...].reshape(256, 128)
    base = math.tanh(sharpness * threshold)
    denominator = base + math.tanh(sharpness * (1.0 - threshold))
    inner = jnp.tanh(sharpness * (filtered - threshold))
    physical = (base + inner) / denominator
    steep = sharpness * (1.0 - inner * inner) / denominator
    inverse = 1.0 / (ramp_shape + physical)
    damp[...] = (damping_max * ramp_shape * (1.0 - physical) * inverse).reshape(16, 16, 128)
    chain[...] = (
        (-damping_max * ramp_shape * (1.0 + ramp_shape)) * steep * inverse * inverse
    ).reshape(16, 16, 128)

    source_own = chain[...] * lean[...]
    raw[...] = source_own
    own_side[...] = dot(source_own.reshape(256, 128), own_taps).reshape(16, 16, 128)
    arrive(faces)

    changes = []
    for side in range(2):
        members = plus_x if side else minus_x
        i = 15 if side else 0
        come = [halo_x[side, k, 8 + velocity[q][1] : 24 + velocity[q][1], :] for k, q in enumerate(members)]
        change = None
        for axis in range(3):
            part = add_all([(velocity[q][axis], come[k]) for k, q in enumerate(members) if velocity[q][axis]])
            part = motion[1 + axis, i, :, :] * part
            change = part if change is None else change + part
        change = -chain[i, :, :] * change
        raw[i, :, :] = raw[i, :, :] + change
        changes.append(change)
    for side in range(2):
        members = plus_y if side else minus_y
        row = 15 if side else 0
        come = [halo_y[side, k, 8 + velocity[q][0] : 24 + velocity[q][0], :] for k, q in enumerate(members)]
        change = None
        for axis in range(3):
            part = add_all([(velocity[q][axis], come[k]) for k, q in enumerate(members) if velocity[q][axis]])
            part = motion[1 + axis, :, row, :] * part
            change = part if change is None else change + part
        change = -chain[:, row, :] * change
        raw[:, row, :] = raw[:, row, :] + change
        changes.append(change)
    swap_raw = [remote(raw, raw_beside, 0, 0, 1)]
    start(swap_raw)
    turned = dot(jnp.concatenate(changes, axis=0), own_taps)
    own_side[0, :, :] = own_side[0, :, :] + turned[0:16]
    own_side[15, :, :] = own_side[15, :, :] + turned[16:32]
    own_side[:, 0, :] = own_side[:, 0, :] + turned[32:48]
    own_side[:, 15, :] = own_side[:, 15, :] + turned[48:64]
    grad_group = slabs(own_side, grad)
    start(grad_group)
    arrive(swap_raw)
    edge_group = join(own_side, raw_beside, grad, edge_out, edges)
    start(edge_group)
    for side in range(2):
        for k in range(5):
            q = (plus_x if side else minus_x)[k]
            padded[q, 17 if side else 0, 8:24, :] = halo_x[side, k, 8:24, :]
            q = (plus_y if side else minus_y)[k]
            padded[q, 1:17, 24 if side else 7, :] = halo_y[side, k, 8:24, :]
    for q in (7, 8, 9, 10):
        side, k, row = corner(q)
        padded[q, 17 if side else 0, row, :] = halo_x[side, k, row, :]

    def collide_step(i, carry):
        for half in range(2):
            rows = pl.ds(8 * half, 8)
            p = [pulled_at(q, i, half) for q in range(Q)]
            scale = motion[0, i, rows, :]
            vel = [motion[1 + a, i, rows, :] for a in range(3)]
            speed_sq = motion[4, i, rows, :]
            damping = damp[i, rows, :]
            cell = label[i, rows, :]
            wp = [lattice_weight[q] * p[q] for q in range(Q)]
            zeroth = add_all([(1, wp[q]) for q in range(Q)])
            first_m = [
                add_all([(velocity[q][a], wp[q]) for q in range(Q) if velocity[q][a]])
                for a in range(3)
            ]
            second = {}
            for a in range(3):
                for b in range(a, 3):
                    second[a, b] = second[b, a] = add_all(
                        [
                            (velocity[q][a] * velocity[q][b], wp[q])
                            for q in range(Q)
                            if velocity[q][a] * velocity[q][b]
                        ]
                    )
            turned = [
                second[a, 0] * vel[0] + second[a, 1] * vel[1] + second[a, 2] * vel[2]
                for a in range(3)
            ]
            quadric = vel[0] * turned[0] + vel[1] * turned[1] + vel[2] * turned[2]
            eq_scalar = zeroth * (1.0 + 1.5 * speed_sq) - 4.5 * quadric
            eq_vector = [
                3.0 * first_m[a] + 9.0 * turned[a] - 3.0 * zeroth * vel[a] for a in range(3)
            ]
            drag = 2.0 * damping * scale
            fluid, solid, inlet = cell == 0, cell == 1, cell == 2
            for q in range(Q):
                c = velocity[q]
                parts = [(c[a], eq_vector[a]) for a in range(3) if c[a]]
                along_eq = add_all([(1, eq_scalar)] + parts) if parts else eq_scalar
                parts = [(c[a], vel[a]) for a in range(3) if c[a]]
                push = add_all(parts) - speed_sq if parts else -speed_sq
                moved = (1.0 - relax_rate) * p[q] + relax_rate * along_eq + drag * push
                value = jnp.where(
                    fluid,
                    moved,
                    jnp.where(solid, p[opposite[q]], jnp.where(inlet, along_eq, eq_scalar)),
                )
                out[q, i, rows, :] = value
        return carry

    lax.fori_loop(0, 16, collide_step, 0)

    arrive(grad_group)
    arrive(edge_group)
    for group in (design_group, faces, z_faces, swap, field_group, swap_raw, grad_group, edge_group):
        sent(group)


def final_kernel(next_in, grad, edges, next_out, sensitivity, middle, result, sems):
    whole = pltpu.make_async_copy(next_in, next_out, sems.at[0])
    whole.start()
    filter_xy(grad, edges, middle, result)
    last = pltpu.make_async_copy(result, sensitivity, sems.at[1])
    last.start()
    last.wait()
    whole.wait()


N_COPIES = 64


def local(forward, adjoint, design, mask):
    block = design.shape
    wide = (32, 32, 128)
    anywhere = pl.BlockSpec(memory_space=pl.ANY)
    in_vmem = pl.BlockSpec(memory_space=pltpu.VMEM)
    vmem = lambda shape, dtype=F32: pltpu.VMEM(shape, dtype)
    nxt, grad, edges = pl.pallas_call(
        main_kernel,
        out_shape=(vmem((Q,) + block), vmem(wide), vmem((8, 8, 128))),
        in_specs=[anywhere] * 4,
        out_specs=(in_vmem,) * 3,
        scratch_shapes=[
            vmem((Q, 18, 32, 128)),
            vmem((5,) + block),
            vmem((2, 5, 16, 128)),
            vmem((2, 5, 16, 128)),
            vmem((2, 5, 32, 128)),
            vmem((2, 5, 32, 128)),
            vmem((Q,) + block),
            vmem(block, jnp.int32),
            vmem(block),
            vmem(block),
            vmem(block),
            vmem(wide),
            vmem((4, 8, 128)),
            vmem((8, 8, 128)),
            vmem((16, 32, 128)),
            vmem(block),
            vmem((5,) + block),
            vmem(block),
            vmem(block),
            vmem(block),
            vmem(block),
            vmem(block),
            vmem(block),
            vmem((4, 8, 128)),
            pltpu.SemaphoreType.DMA((4,)),
            pltpu.SemaphoreType.DMA((N_COPIES,)),
            pltpu.SemaphoreType.DMA((N_COPIES,)),
        ],
        compiler_params=pltpu.CompilerParams(collective_id=0, has_side_effects=True),
        name="adjoint_main",
    )(forward, adjoint, design, mask)
    keep = lambda a: pltpu.with_memory_space_constraint(a, pltpu.VMEM)
    return pl.pallas_call(
        final_kernel,
        out_shape=(
            jax.ShapeDtypeStruct((Q,) + block, F32),
            jax.ShapeDtypeStruct(block, F32),
        ),
        in_specs=[in_vmem] * 3,
        out_specs=(anywhere, anywhere),
        scratch_shapes=[
            vmem((16, 32, 128)),
            vmem(block),
            pltpu.SemaphoreType.DMA((2,)),
        ],
        name="adjoint_final",
    )(keep(nxt), keep(grad), keep(edges))


def solution(mesh):
    return jax.shard_map(
        local,
        mesh=mesh,
        in_specs=(
            P(None, "gx", "gy", "gz"),
            P(None, "gx", "gy", "gz"),
            P("gx", "gy", "gz"),
            P("gx", "gy", "gz"),
        ),
        out_specs=(P(None, "gx", "gy", "gz"), P("gx", "gy", "gz")),
        check_vma=False,
    )
```

```python
import functools
import math

import jax
import jax.numpy as jnp
from jax import lax
from jax.experimental import pallas as pl
from jax.experimental.pallas import tpu as pltpu
from jax.sharding import PartitionSpec as P

Q = 19
RADIUS = 8
MESH = pl.DeviceIdType.MESH
F32 = jnp.float32

velocity = [
    (0, 0, 0),
    (1, 0, 0),
    (-1, 0, 0),
    (0, 1, 0),
    (0, -1, 0),
    (0, 0, 1),
    (0, 0, -1),
    (1, 1, 0),
    (-1, -1, 0),
    (1, -1, 0),
    (-1, 1, 0),
    (1, 0, 1),
    (-1, 0, -1),
    (1, 0, -1),
    (-1, 0, 1),
    (0, 1, 1),
    (0, -1, -1),
    (0, 1, -1),
    (0, -1, 1),
]
lattice_weight = [1.0 / 3.0] + [1.0 / 18.0] * 6 + [1.0 / 36.0] * 12
opposite = [0, 2, 1, 4, 3, 6, 5, 8, 7, 10, 9, 12, 11, 14, 13, 16, 15, 18, 17]
relax_rate = 1.25
sharpness = 64.0
threshold = 0.5
damping_max = 10.0
ramp_shape = 0.1

slot_of = {5: 0, 6: 0, 11: 1, 12: 1, 14: 2, 13: 2, 15: 3, 16: 3, 18: 4, 17: 4}

unscaled = [math.exp(-(k * k) / (2.0 * (RADIUS / 2.0) ** 2)) for k in range(RADIUS + 1)]
tap_sum = unscaled[0] + 2.0 * sum(unscaled[1:])
TAPS = [v / tap_sum for v in unscaled]


def tap_matrix(offset):
    row = lax.broadcasted_iota(jnp.int32, (128, 128), 0)
    col = lax.broadcasted_iota(jnp.int32, (128, 128), 1)
    gap = jnp.abs(row + offset - col)
    result = jnp.zeros((128, 128), F32)
    for k in range(RADIUS + 1):
        result = jnp.where(gap == k, TAPS[k], result)
    return result


def symmetric(take):
    total = TAPS[0] * take(0)
    for k in range(1, RADIUS + 1):
        total = total + TAPS[k] * (take(k) + take(-k))
    return total


def filter_xy(source, edges, middle, result):
    Z = lax.axis_index("gz")
    lane = lax.broadcasted_iota(jnp.int32, (8, 128), 1)
    lowest = 120 * (1 - Z)
    edge = jnp.logical_and(lane >= lowest, lane < lowest + 8)

    def spread(n, u):
        whole_row = edges[n, :, :]
        if u:
            whole_row = pltpu.roll(whole_row, 128 - 8 * u, 1)
        return jnp.where(edge, whole_row, 0.0)

    for group in range(4):
        rows = slice(8 * group, 8 * group + 8)
        dy = 1 if group == 0 else -1 if group == 3 else 0
        planes = []
        for i in range(32):
            plane = source[i, rows, :]
            dx = 1 if i < 8 else -1 if i >= 24 else 0
            if dx or dy:
                if dx == 0:
                    u = i - 8
                else:
                    u = 2 * (i % 8) + (group - 1 if dy == 0 else 1 if dy > 0 else 0)
                plane = plane + spread(ORDER.index((dx, dy)), u)
            planes.append(plane)
        for i in range(16):
            middle[i, rows, :] = symmetric(lambda k: planes[i + 8 + k])
    filter_y(middle, result)


def filter_y(middle, result):
    def along_y(i, carry):
        rows = [middle[i, pl.ds(at, 8), :] for at in range(25)]
        for half in range(2):
            result[i, pl.ds(8 * half, 8), :] = symmetric(lambda k: rows[8 + 8 * half + k])
        return carry

    lax.fori_loop(0, 16, along_y, 0)


ORDER = [(1, 0), (-1, 0), (1, 1), (1, -1), (-1, 1), (-1, -1), (0, 1), (0, -1)]


def packed(units):
    total = units[0]
    for u in range(1, 16):
        total = total + pltpu.roll(units[u], 8 * u, 1)
    return total


def dot(a, b):
    return jnp.dot(a, b, precision=lax.Precision.HIGHEST, preferred_element_type=F32)


def add_all(members):
    total = None
    for sign, member in members:
        if total is None:
            total = member if sign > 0 else -member
        else:
            total = total + member if sign > 0 else total - member
    return total


def main_kernel(
    forward,
    adjoint,
    design,
    mask,
    out,
    grad,
    edges,
    padded,
    beside,
    face_x,
    face_y,
    halo_x,
    halo_y,
    flow,
    label,
    plain,
    own_design,
    design_beside,
    field,
    field_out,
    field_edges,
    middle,
    smoothed,
    motion,
    chain,
    damp,
    raw,
    raw_beside,
    lean,
    own_side,
    edge_out,
    local_sem,
    send_sem,
    recv_sem,
):
    nx, ny = lax.axis_size("gx"), lax.axis_size("gy")
    X, Y, Z = lax.axis_index("gx"), lax.axis_index("gy"), lax.axis_index("gz")
    low_x, high_x = X > 0, X < nx - 1
    low_y, high_y = Y > 0, Y < ny - 1

    def exists(dx, dy):
        found = True
        if dx:
            found = high_x if dx > 0 else low_x
        if dy:
            found_y = high_y if dy > 0 else low_y
            found = found_y if found is True else jnp.logical_and(found, found_y)
        return found

    def when(cond, body):
        if cond is True:
            body()
        else:
            pl.when(cond)(body)

    def device(dx, dy, other):
        return (X + dx, Y + dy, 1 - Z if other else Z)

    loads = [
        pltpu.make_async_copy(design, plain, local_sem.at[0]),
        pltpu.make_async_copy(forward, flow, local_sem.at[1]),
        pltpu.make_async_copy(adjoint, padded.at[:, 1:17, 8:24, :], local_sem.at[2]),
        pltpu.make_async_copy(mask, label, local_sem.at[3]),
    ]
    for load in loads:
        load.start()

    around = [(dx, dy, 0) for dx in (-1, 0, 1) for dy in (-1, 0, 1) if dx or dy]
    around.append((0, 0, 1))
    barrier = pltpu.get_barrier_semaphore()
    for dx, dy, other in around:
        when(
            exists(dx, dy),
            lambda: pl.semaphore_signal(
                barrier, inc=1, device_id=device(dx, dy, other), device_id_type=MESH
            ),
        )

    plus_x = [q for q in range(Q) if velocity[q][0] > 0]
    minus_x = [q for q in range(Q) if velocity[q][0] < 0]
    plus_y = [q for q in range(Q) if velocity[q][1] > 0]
    minus_y = [q for q in range(Q) if velocity[q][1] < 0]

    for q in minus_x + plus_x:
        padded[q, 17 if q in plus_x else 0, :, :] = jnp.zeros((32, 128), F32)
    for q in minus_y + plus_y:
        padded[q, 1:17, 24 if q in plus_y else 7, :] = jnp.zeros((16, 128), F32)
    for side in range(2):
        for k in range(5):
            for row in (7, 24):
                halo_y[side, k, row : row + 1, :] = jnp.zeros((1, 128), F32)

    def clear_x(side):
        halo_x[max(side, 0), :, 8:24, :] = jnp.zeros((5, 16, 128), F32)
        begin = 0 if side < 0 else 24
        for ref in (field, grad):
            ref[begin : begin + 8, :, :] = jnp.zeros((8, 32, 128), F32)

    def clear_y(side):
        halo_y[max(side, 0), :, 8:24, :] = jnp.zeros((5, 16, 128), F32)
        begin = 0 if side < 0 else 24
        for ref in (field, grad):
            ref[:, begin : begin + 8, :] = jnp.zeros((32, 8, 128), F32)

    def corner(q):
        cx, cy, cz = velocity[q]
        k = (plus_x if cx > 0 else minus_x).index(q)
        return (1 if cx > 0 else 0), k, slice(24, 25) if cy > 0 else slice(7, 8)

    def clear_corner(q):
        side, k, row = corner(q)
        halo_x[side, k, row, :] = jnp.zeros((1, 128), F32)

    def clear_edge(n):
        for ref in (edges, field_edges):
            ref[n, :, :] = jnp.zeros((8, 128), F32)

    for n, (dx, dy) in enumerate(ORDER):
        when(jnp.logical_not(exists(-dx, -dy)), lambda: clear_edge(n))
    for q in (7, 8, 9, 10):
        cx, cy, cz = velocity[q]
        when(jnp.logical_not(exists(cx, cy)), lambda: clear_corner(q))
    for side in (-1, 1):
        when(jnp.logical_not(exists(side, 0)), lambda: clear_x(side))
        when(jnp.logical_not(exists(0, side)), lambda: clear_y(side))

    own_taps = tap_matrix(0)
    beside_taps = tap_matrix(jnp.where(Z == 0, 128, -128))
    loads[0].wait()
    own_design[...] = dot(plain[...].reshape(256, 128), own_taps).reshape(16, 16, 128)
    sides_x = jnp.where(low_x, 1, 0) + jnp.where(high_x, 1, 0)
    sides_y = jnp.where(low_y, 1, 0) + jnp.where(high_y, 1, 0)
    pl.semaphore_wait(barrier, 1 + sides_x + sides_y + sides_x * sides_y)

    count = [0]

    def remote(src, dst, dx, dy, other, extra=None):
        copy = pltpu.make_async_remote_copy(
            src_ref=src,
            dst_ref=dst,
            send_sem=send_sem.at[count[0]],
            recv_sem=recv_sem.at[count[0]],
            device_id=device(dx, dy, other),
            device_id_type=MESH,
        )
        count[0] += 1
        return (exists(dx, dy), exists(-dx, -dy), copy, extra)

    def both(cond, extra):
        if extra is None:
            return cond
        return extra if cond is True else jnp.logical_and(cond, extra)

    def start(group):
        for sends, _, copy, extra in group:
            when(both(sends, extra and extra[0]), copy.start)

    def arrive(group):
        for _, receives, copy, extra in group:
            when(both(receives, extra and extra[1]), copy.wait_recv)

    def sent(group):
        for sends, _, copy, extra in group:
            when(both(sends, extra and extra[0]), copy.wait_send)

    def slab(ref, dx, dy):
        def own(d):
            return slice(8, 16) if d > 0 else slice(0, 8) if d < 0 else slice(0, 16)

        return ref.at[own(dx), own(dy), :]

    def halo(ref, dx, dy):
        def there(d):
            return slice(0, 8) if d > 0 else slice(24, 32) if d < 0 else slice(8, 24)

        return ref.at[there(dx), there(dy), :]

    def slabs(own, result):
        return [remote(slab(own, dx, dy), halo(result, dx, dy), dx, dy, 0) for dx, dy in ORDER]

    def join(own, received, result, packs, landing):
        other = dot(received[...].reshape(256, 128), beside_taps).reshape(16, 16, 128)
        result[8:24, 8:24, :] = own[...] + other
        for side in range(2):
            at = 0 if side else 8
            packs[side, :, :] = packed(
                [other[at + p, 8 * g : 8 * g + 8, :] for p in range(8) for g in range(2)]
            )
            packs[2 + side, :, :] = packed([other[i, at : at + 8, :] for i in range(16)])
        return [
            remote(
                packs.at[(0 if dx > 0 else 1) if dx else (2 if dy > 0 else 3)],
                landing.at[n],
                dx,
                dy,
                0,
            )
            for n, (dx, dy) in enumerate(ORDER)
        ]

    swap = [remote(design, design_beside, 0, 0, 1)]
    design_group = slabs(own_design, field)
    corners = []
    for q in (7, 8, 9, 10):
        cx, cy, cz = velocity[q]
        side, k, row = corner(q)
        corners.append(
            remote(
                adjoint.at[q, 0 if cx > 0 else 15, slice(0, 1) if cy > 0 else slice(15, 16), :],
                halo_x.at[side, k, row, :],
                -cx,
                -cy,
                0,
            )
        )
    start(swap)
    start(corners)
    start(design_group)

    z_faces = [
        remote(adjoint.at[q * Z + opposite[q] * (1 - Z)], beside.at[slot_of[q]], 0, 0, 1)
        for q in (5, 11, 14, 15, 18)
    ]
    start(z_faces)

    arrive(swap)
    field_group = join(own_design, design_beside, field, field_out, field_edges)
    start(field_group)

    lane = lax.broadcasted_iota(jnp.int32, (16, 128), 1)
    first, last = lane == 0, lane == 127
    first_open = lane == -Z
    last_open = lane == 128 * Z - 1
    loads[2].wait()
    arrive(z_faces)

    def pull_z(i, carry):
        for q in slot_of:
            own = padded[q, i + 1, 8:24, :]
            edge = beside[slot_of[q], i, :, :]
            if velocity[q][2] > 0:
                joined = jnp.where(first, jnp.where(first_open, edge, 0.0), own)
                shifted = pltpu.roll(joined, 127, 1)
            else:
                joined = jnp.where(last, jnp.where(last_open, edge, 0.0), own)
                shifted = pltpu.roll(joined, 1, 1)
            padded[q, i + 1, 8:24, :] = shifted
        return carry

    lax.fori_loop(0, 16, pull_z, 0)
    for k in range(5):
        face_x[0, k, :, :] = padded[minus_x[k], 16, 8:24, :]
        face_x[1, k, :, :] = padded[plus_x[k], 1, 8:24, :]
        face_y[0, k, :, :] = padded[minus_y[k], 1:17, 23, :]
        face_y[1, k, :, :] = padded[plus_y[k], 1:17, 8, :]
    faces = [
        remote(face_x.at[0], halo_x.at[0, :, 8:24, :], 1, 0, 0),
        remote(face_x.at[1], halo_x.at[1, :, 8:24, :], -1, 0, 0),
        remote(face_y.at[0], halo_y.at[0, :, 8:24, :], 0, 1, 0),
        remote(face_y.at[1], halo_y.at[1, :, 8:24, :], 0, -1, 0),
    ]
    start(faces)

    loads[1].wait()

    def flow_step(i, carry):
        for half in range(2):
            rows = pl.ds(8 * half, 8)
            f = [flow[q, i, rows, :] for q in range(Q)]
            scale = 1.0 / add_all([(1, f[q]) for q in range(Q)])
            vel = [
                add_all([(velocity[q][a], f[q]) for q in range(Q) if velocity[q][a]]) * scale
                for a in range(3)
            ]
            motion[0, i, rows, :] = scale
            for a in range(3):
                motion[1 + a, i, rows, :] = vel[a]
            motion[4, i, rows, :] = vel[0] * vel[0] + vel[1] * vel[1] + vel[2] * vel[2]
        return carry

    lax.fori_loop(0, 16, flow_step, 0)


    def pulled_at(q, i, half):
        cx, cy, cz = velocity[q]
        return padded[q, i + (1 + cx), pl.ds(8 + 8 * half + cy, 8), :]

    def moment_step(i, carry):
        for half in range(2):
            rows = pl.ds(8 * half, 8)
            p = [None] + [pulled_at(q, i, half) for q in range(1, Q)]
            total = motion[4, i, rows, :]
            for axis in range(3):
                moment = add_all([(velocity[q][axis], p[q]) for q in range(1, Q) if velocity[q][axis]])
                total = total - motion[1 + axis, i, rows, :] * moment
            lean[i, rows, :] = total
        return carry

    lax.fori_loop(0, 16, moment_step, 0)
    arrive(design_group)
    arrive(field_group)
    filter_xy(field, field_edges, middle, smoothed)
    loads[3].wait()
    filtered = smoothed[...].reshape(256, 128)
    base = math.tanh(sharpness * threshold)
    denominator = base + math.tanh(sharpness * (1.0 - threshold))
    inner = jnp.tanh(sharpness * (filtered - threshold))
    physical = (base + inner) / denominator
    steep = sharpness * (1.0 - inner * inner) / denominator
    inverse = 1.0 / (ramp_shape + physical)
    damp[...] = (damping_max * ramp_shape * (1.0 - physical) * inverse).reshape(16, 16, 128)
    chain[...] = (
        (-damping_max * ramp_shape * (1.0 + ramp_shape)) * steep * inverse * inverse
    ).reshape(16, 16, 128)

    source_own = chain[...] * lean[...]
    raw[...] = source_own
    own_side[...] = dot(source_own.reshape(256, 128), own_taps).reshape(16, 16, 128)
    arrive(corners)
    arrive(faces)

    changes = []
    for side in range(2):
        members = plus_x if side else minus_x
        i = 15 if side else 0
        come = [halo_x[side, k, 8 + velocity[q][1] : 24 + velocity[q][1], :] for k, q in enumerate(members)]
        change = None
        for axis in range(3):
            part = add_all([(velocity[q][axis], come[k]) for k, q in enumerate(members) if velocity[q][axis]])
            part = motion[1 + axis, i, :, :] * part
            change = part if change is None else change + part
        change = -chain[i, :, :] * change
        raw[i, :, :] = raw[i, :, :] + change
        changes.append(change)
    for side in range(2):
        members = plus_y if side else minus_y
        row = 15 if side else 0
        come = [halo_y[side, k, 8 + velocity[q][0] : 24 + velocity[q][0], :] for k, q in enumerate(members)]
        change = None
        for axis in range(3):
            part = add_all([(velocity[q][axis], come[k]) for k, q in enumerate(members) if velocity[q][axis]])
            part = motion[1 + axis, :, row, :] * part
            change = part if change is None else change + part
        change = -chain[:, row, :] * change
        raw[:, row, :] = raw[:, row, :] + change
        changes.append(change)
    swap_raw = [remote(raw, raw_beside, 0, 0, 1)]
    start(swap_raw)
    turned = dot(jnp.concatenate(changes, axis=0), own_taps)
    own_side[0, :, :] = own_side[0, :, :] + turned[0:16]
    own_side[15, :, :] = own_side[15, :, :] + turned[16:32]
    own_side[:, 0, :] = own_side[:, 0, :] + turned[32:48]
    own_side[:, 15, :] = own_side[:, 15, :] + turned[48:64]
    grad_group = slabs(own_side, grad)
    start(grad_group)
    arrive(swap_raw)
    edge_group = join(own_side, raw_beside, grad, edge_out, edges)
    start(edge_group)
    for side in range(2):
        for k in range(5):
            q = (plus_x if side else minus_x)[k]
            padded[q, 17 if side else 0, 8:24, :] = halo_x[side, k, 8:24, :]
            q = (plus_y if side else minus_y)[k]
            padded[q, 1:17, 24 if side else 7, :] = halo_y[side, k, 8:24, :]
    for q in (7, 8, 9, 10):
        side, k, row = corner(q)
        padded[q, 17 if side else 0, row, :] = halo_x[side, k, row, :]

    def collide_step(i, carry):
        for half in range(2):
            rows = pl.ds(8 * half, 8)
            p = [pulled_at(q, i, half) for q in range(Q)]
            scale = motion[0, i, rows, :]
            vel = [motion[1 + a, i, rows, :] for a in range(3)]
            speed_sq = motion[4, i, rows, :]
            damping = damp[i, rows, :]
            cell = label[i, rows, :]
            wp = [lattice_weight[q] * p[q] for q in range(Q)]
            zeroth = add_all([(1, wp[q]) for q in range(Q)])
            first_m = [
                add_all([(velocity[q][a], wp[q]) for q in range(Q) if velocity[q][a]])
                for a in range(3)
            ]
            second = {}
            for a in range(3):
                for b in range(a, 3):
                    second[a, b] = second[b, a] = add_all(
                        [
                            (velocity[q][a] * velocity[q][b], wp[q])
                            for q in range(Q)
                            if velocity[q][a] * velocity[q][b]
                        ]
                    )
            turned = [
                second[a, 0] * vel[0] + second[a, 1] * vel[1] + second[a, 2] * vel[2]
                for a in range(3)
            ]
            quadric = vel[0] * turned[0] + vel[1] * turned[1] + vel[2] * turned[2]
            eq_scalar = zeroth * (1.0 + 1.5 * speed_sq) - 4.5 * quadric
            eq_vector = [
                3.0 * first_m[a] + 9.0 * turned[a] - 3.0 * zeroth * vel[a] for a in range(3)
            ]
            drag = 2.0 * damping * scale
            fluid, solid, inlet = cell == 0, cell == 1, cell == 2
            for q in range(Q):
                c = velocity[q]
                parts = [(c[a], eq_vector[a]) for a in range(3) if c[a]]
                along_eq = add_all([(1, eq_scalar)] + parts) if parts else eq_scalar
                parts = [(c[a], vel[a]) for a in range(3) if c[a]]
                push = add_all(parts) - speed_sq if parts else -speed_sq
                moved = (1.0 - relax_rate) * p[q] + relax_rate * along_eq + drag * push
                value = jnp.where(
                    fluid,
                    moved,
                    jnp.where(solid, p[opposite[q]], jnp.where(inlet, along_eq, eq_scalar)),
                )
                out[q, i, rows, :] = value
        return carry

    lax.fori_loop(0, 16, collide_step, 0)

    arrive(grad_group)
    arrive(edge_group)
    for group in (design_group, corners, faces, z_faces, swap, field_group, swap_raw, grad_group, edge_group):
        sent(group)


def final_kernel(next_in, grad, edges, next_out, sensitivity, middle, result, sems):
    whole = pltpu.make_async_copy(next_in, next_out, sems.at[0])
    whole.start()
    filter_xy(grad, edges, middle, result)
    last = pltpu.make_async_copy(result, sensitivity, sems.at[1])
    last.start()
    last.wait()
    whole.wait()


N_COPIES = 64


def local(forward, adjoint, design, mask):
    block = design.shape
    wide = (32, 32, 128)
    anywhere = pl.BlockSpec(memory_space=pl.ANY)
    in_vmem = pl.BlockSpec(memory_space=pltpu.VMEM)
    vmem = lambda shape, dtype=F32: pltpu.VMEM(shape, dtype)
    nxt, grad, edges = pl.pallas_call(
        main_kernel,
        out_shape=(vmem((Q,) + block), vmem(wide), vmem((8, 8, 128))),
        in_specs=[anywhere] * 4,
        out_specs=(in_vmem,) * 3,
        scratch_shapes=[
            vmem((Q, 18, 32, 128)),
            vmem((5,) + block),
            vmem((2, 5, 16, 128)),
            vmem((2, 5, 16, 128)),
            vmem((2, 5, 32, 128)),
            vmem((2, 5, 32, 128)),
            vmem((Q,) + block),
            vmem(block, jnp.int32),
            vmem(block),
            vmem(block),
            vmem(block),
            vmem(wide),
            vmem((4, 8, 128)),
            vmem((8, 8, 128)),
            vmem((16, 32, 128)),
            vmem(block),
            vmem((5,) + block),
            vmem(block),
            vmem(block),
            vmem(block),
            vmem(block),
            vmem(block),
            vmem(block),
            vmem((4, 8, 128)),
            pltpu.SemaphoreType.DMA((4,)),
            pltpu.SemaphoreType.DMA((N_COPIES,)),
            pltpu.SemaphoreType.DMA((N_COPIES,)),
        ],
        compiler_params=pltpu.CompilerParams(collective_id=0, has_side_effects=True),
        name="adjoint_main",
    )(forward, adjoint, design, mask)
    keep = lambda a: pltpu.with_memory_space_constraint(a, pltpu.VMEM)
    return pl.pallas_call(
        final_kernel,
        out_shape=(
            jax.ShapeDtypeStruct((Q,) + block, F32),
            jax.ShapeDtypeStruct(block, F32),
        ),
        in_specs=[in_vmem] * 3,
        out_specs=(anywhere, anywhere),
        scratch_shapes=[
            vmem((16, 32, 128)),
            vmem(block),
            pltpu.SemaphoreType.DMA((2,)),
        ],
        name="adjoint_final",
    )(keep(nxt), keep(grad), keep(edges))


def solution(mesh):
    return jax.shard_map(
        local,
        mesh=mesh,
        in_specs=(
            P(None, "gx", "gy", "gz"),
            P(None, "gx", "gy", "gz"),
            P("gx", "gy", "gz"),
            P("gx", "gy", "gz"),
        ),
        out_specs=(P(None, "gx", "gy", "gz"), P("gx", "gy", "gz")),
        check_vma=False,
    )
```
